32 devices in a mesh: row: 4 (over y, x), col: 4 (over z), vox: 2 (over core).
Axes of the slice: x: 2, y: 2, z: 4, core: 2. Of those that a mesh axis runs over, the one named last changes fastest.
Arguments:
- coeffs_r: bfloat16 [32, 4, 64, 2, 1024], P(None, 'row', None, None, 'col'), may hold values from -0.125 to 0.125
- rhs: bfloat16 [32, 4, 64, 1536], P('col', 'row', None, 'vox'), may hold values from -6 to 6
- inverses: bfloat16 [2, 1024, 1024], replicated, may hold values from -0.1875 to 0.1875
Outputs:
- updated: bfloat16 [32, 4, 64, 1536], P('col', 'row', None, 'vox')
The draws below stay inside these ranges and needn't reach their ends.
All inputs are finite; a program needn't handle non-finite values.
Results may differ from the reference program's by a relative error of at most 0.0049.
Values may be sent and summed in bfloat16 or wider, within the bound.
No kernel may reach another device: no remote copies, remote signals or barrier semaphores. Data moves between devices by JAX's collectives and lax.ppermute only.
A program may use at most 64 MiB of HBM per device.

```python
import jax
import jax.numpy as jnp

NB = 1024
VOX = 1536
RB = 64
RGRID = 4
CYC = 32


def level_of(rng, dims, pieces, smallest, high):
    def one(position, shards_of):
        heights = jax.random.uniform(jax.random.fold_in(jax.random.fold_in(rng, 6), position), (shards_of,), jnp.float32, smallest / len(pieces), high / len(pieces))
        return jnp.repeat(jnp.exp(heights), dims[position] // shards_of).reshape((-1,) + (1,) * (len(dims) - position - 1))

    gain = one(*pieces[0])
    for cut in pieces[1:]:
        gain = gain * one(*cut)
    return gain


def scatter_about(own_key, dims, spread, reach, shards=(), held_as=jnp.bfloat16):
    loudness = level_of(own_key, dims, shards, -0.22, 0.18) if shards else 1.0
    result = jax.random.normal(own_key, dims, jnp.float32) * spread * loudness
    return jnp.minimum(jnp.maximum(result, -reach), reach).astype(held_as)


def setup_inputs(seed: int = 0) -> dict:
    splits = jax.random.split(jax.random.key(seed), 4)
    coeffs_r = scatter_about(splits[0], (CYC, RGRID, RB, 2, NB), (2 * NB) ** -0.5, 0.125, ((1, 4), (4, 4)))
    rhs = scatter_about(splits[1], (CYC, RGRID, RB, VOX), 1.0, 6.0, ((0, 4), (1, 4), (3, 2)))
    inverses = scatter_about(splits[2], (2, NB, NB), NB ** -0.5, 0.1875)
    return dict(coeffs_r=coeffs_r, rhs=rhs, inverses=inverses)


def reference(coeffs_r, rhs, inverses):
    order = CYC * RGRID * RB
    factor = coeffs_r.reshape(order, 2, NB)
    right = rhs.reshape(order, VOX)
    top = order - 2 * NB
    x_last = jnp.dot(inverses[1], right[order - NB:], preferred_element_type=jnp.float32).astype(jnp.bfloat16)
    mid_rhs = right[top:order - NB].astype(jnp.float32) - jnp.dot(factor[top:order - NB, 1], x_last, preferred_element_type=jnp.float32)
    mid_rhs = mid_rhs.astype(jnp.bfloat16)
    x_mid = jnp.dot(inverses[0], mid_rhs, preferred_element_type=jnp.float32).astype(jnp.bfloat16)
    remaining = right[:top].astype(jnp.float32) - jnp.dot(factor[:top, 0], x_mid, preferred_element_type=jnp.float32)
    remaining = remaining - jnp.dot(factor[:top, 1], x_last, preferred_element_type=jnp.float32)
    joined = jnp.concatenate([remaining.astype(jnp.bfloat16), x_mid, x_last], 0)
    return joined.reshape(CYC, RGRID, RB, VOX)
```

```python
import jax
import jax.numpy as jnp
from jax import lax
from jax.sharding import PartitionSpec as P


def local(coeffs_r, rhs, inverses):
    row_count = lax.axis_size("row")
    col_count = lax.axis_size("col")
    vox_count = lax.axis_size("vox")
    row_pos = lax.axis_index("row")
    col_pos = lax.axis_index("col")
    vox_pos = lax.axis_index("vox")
    per_col = rhs.shape[0]
    block_rows = rhs.shape[2]
    voxels = rhs.shape[3]
    own_cols = coeffs_r.shape[4]
    order = inverses.shape[1]
    cycles = coeffs_r.shape[0]
    tail = order // (block_rows * row_count)
    piece = tail * block_rows
    owner = col_count - 1
    zero = jnp.zeros((), jnp.int32)

    def gather_rows(value, cols):
        v = value.shape[1]
        full = jnp.zeros((tail, row_count, block_rows, v), value.dtype)
        for d in range(row_count):
            if d == 0:
                got = value
            else:
                pairs = [
                    (r * col_count + c, (r ^ d) * col_count + c)
                    for r in range(row_count)
                    for c in cols
                ]
                got = lax.ppermute(value, ("row", "col"), pairs)
            full = lax.dynamic_update_slice(
                full, got.reshape(tail, 1, block_rows, v), (zero, row_pos ^ d, zero, zero)
            )
        return full.reshape(order, v)

    def down(value):
        stride = col_count // 2
        holders = [owner]
        while stride:
            pairs = [(h, h - stride) for h in holders]
            got = lax.ppermute(value, "col", pairs)
            is_target = jnp.zeros((), bool)
            for _, t in pairs:
                is_target = is_target | (col_pos == t)
            value = jnp.where(is_target, got, value)
            holders = holders + [t for _, t in pairs]
            stride //= 2
        return value

    mid_piece = rhs[per_col - 2 * tail : per_col - tail].reshape(piece, voxels)
    last_piece = rhs[per_col - tail :].reshape(piece, voxels)
    last_top = gather_rows(last_piece, [owner])
    panel = coeffs_r[cycles - 2 * tail : cycles - tail, 0, :, 1, :].reshape(piece, own_cols)
    panels = [lax.ppermute(panel, "col", [(c, owner)]) for c in range(owner)] + [panel]
    last_full = gather_rows(down(last_piece), list(range(owner)))
    last_full = jnp.where(col_pos == owner, last_top, last_full)

    half = per_col // vox_count
    split = coeffs_r.reshape(col_count, vox_count, half, block_rows, 2, own_cols)
    mine = lax.dynamic_slice_in_dim(split, vox_pos, 1, 1).reshape(
        col_count, half, block_rows, 2, own_cols
    )
    mine = lax.all_to_all(mine, "col", 0, 0, tiled=True)
    other = lax.ppermute(mine, "vox", [(0, 1), (1, 0)])
    low = jnp.where(vox_pos == 0, mine, other)
    high = jnp.where(vox_pos == 0, other, mine)
    coeffs = jnp.stack([low, high], 1)
    coeffs = coeffs.transpose(4, 1, 2, 3, 0, 5).reshape(2, per_col * block_rows, order)

    def dot(a, b):
        return jnp.dot(a, b, preferred_element_type=jnp.float32)

    x_top = dot(inverses[1], last_top).astype(jnp.bfloat16)
    mid = mid_piece.astype(jnp.float32) - dot(jnp.concatenate(panels, 1), x_top)
    mid_full = gather_rows(down(mid.astype(jnp.bfloat16)), list(range(col_count)))
    x_last = dot(inverses[1], last_full).astype(jnp.bfloat16)
    flat = rhs.reshape(per_col * block_rows, voxels).astype(jnp.float32) - dot(coeffs[1], x_last)
    x_mid = dot(inverses[0], mid_full).astype(jnp.bfloat16)
    flat = (flat - dot(coeffs[0], x_mid)).astype(jnp.bfloat16)
    remaining = flat.reshape(per_col, 1, block_rows, voxels)

    def my_rows(solved):
        shaped = solved.reshape(tail, row_count, block_rows, voxels)
        return lax.dynamic_slice_in_dim(shaped, row_pos, 1, 1)

    window = jnp.concatenate([my_rows(x_mid), my_rows(x_last)], 0)
    lower = jnp.where(col_pos == owner, window, remaining[per_col - 2 * tail :])
    return jnp.concatenate([remaining[: per_col - 2 * tail], lower], 0)


def solution(mesh):
    placed = (P(None, "row", None, None, "col"), P("col", "row", None, "vox"), P())
    return jax.shard_map(
        local, mesh=mesh, in_specs=placed, out_specs=P("col", "row", None, "vox"), check_vma=False
    )
```

```python
import functools

import jax
import jax.numpy as jnp
from jax import lax
from jax.experimental import pallas as pl
from jax.experimental.pallas import tpu as pltpu
from jax.sharding import PartitionSpec as P

VMEM = pl.BlockSpec(memory_space=pltpu.VMEM)
CHUNKS = 2
SMEM = pl.BlockSpec(memory_space=pltpu.SMEM)


def chunk_bounds(voxels):
    cut = voxels // 256 * 2 // 3 * 256 or voxels // 2
    return [slice(0, cut), slice(cut, voxels)]


def dot(a, b):
    return jnp.dot(a, b, preferred_element_type=jnp.float32)


def assemble(full, pieces, row_pos, rows):
    count = len(pieces)
    tail = pieces[0].shape[0] // rows
    for d, piece in enumerate(pieces):
        p = row_pos ^ d
        for k in range(tail):
            at = pl.multiple_of((k * count + p) * rows, rows)
            full[pl.ds(at, rows), :] = piece[k * rows : (k + 1) * rows, :]


def solve(x, inverses, which, full):
    step = min(256, x.shape[0])

    def body(m, _):
        at = pl.multiple_of(m * step, step)
        x[pl.ds(at, step), :] = dot(inverses[which, pl.ds(at, step), :], full[...]).astype(x.dtype)
        return 0

    lax.fori_loop(0, x.shape[0] // step, body, 0)


def mid_kernel(row_count, rows, start, cols, where, *refs):
    pieces = [ref.at[:, cols] for ref in refs[:row_count]]
    inverses, mine, other, mid, out, full, x = refs[row_count:]
    assemble(full, pieces, where[0], rows)
    solve(x, inverses, 1, full)
    half, piece = mine.shape[1], mid.shape[0]
    for h in range(2):
        low, high = max(start, h * half), min(start + piece, (h + 1) * half)
        if low >= high:
            continue
        to = slice(low - start, high - start)

        def rest(coeffs):
            total = mid[to, cols].astype(jnp.float32)
            total = subtract(total, coeffs, x, slice(low - h * half, high - h * half))
            out[to, :] = total.astype(out.dtype)

        pl.when(where[1] == h)(functools.partial(rest, mine))
        pl.when(where[1] != h)(functools.partial(rest, other))


def subtract(total, coeffs, x, at):
    own = coeffs.shape[2]
    for c in range(coeffs.shape[0]):
        total = total - dot(coeffs[c, at, :], x[c * own : (c + 1) * own, :])
    return total


def own_rows(x, row_pos, count, rows):
    tail = x.shape[0] // (count * rows)
    return [x[pl.ds(pl.multiple_of((k * count + row_pos) * rows, rows), rows), :] for k in range(tail)]


def last_kernel(row_count, rows, where, *refs):
    pieces = refs[:row_count]
    inverses, mine, other, rhs, acc, x_rows, full, x = refs[row_count:]
    assemble(full, pieces, where[0], rows)
    solve(x, inverses, 1, full)
    for k, part in enumerate(own_rows(x, where[0], row_count, rows)):
        x_rows[k * rows : (k + 1) * rows, :] = part
    half = mine.shape[1]
    for coeffs, h in ((mine, where[1]), (other, 1 - where[1])):
        at = pl.multiple_of(h * half, half)
        total = rhs[pl.ds(at, half), :].astype(jnp.float32)
        acc[pl.ds(at, half), :] = subtract(total, coeffs, x, slice(None))


def final_kernel(row_count, rows, chunks, where, *refs):
    pieces = refs[: row_count * chunks]
    inverses, mine, other, acc, x_rows, out, full, x = refs[row_count * chunks :]
    for n, cols in enumerate(chunk_bounds(full.shape[1])):
        assemble(full.at[:, cols], pieces[n::chunks], where[0], rows)
    solve(x, inverses, 0, full)
    half = mine.shape[1]
    for coeffs, h in ((mine, where[1]), (other, 1 - where[1])):
        at = pl.multiple_of(h * half, half)
        total = subtract(acc[pl.ds(at, half), :], coeffs, x, slice(None))
        out[pl.ds(at, half), :] = total.astype(out.dtype)

    @pl.when(where[2] == 1)
    def _():
        piece = x_rows.shape[0]
        start = out.shape[0] - 2 * piece
        for k, part in enumerate(own_rows(x, where[0], row_count, rows)):
            out[start + k * rows : start + (k + 1) * rows, :] = part
        out[start + piece :, :] = x_rows[...]


def local(coeffs_r, rhs, inverses):
    row_count = lax.axis_size("row")
    col_count = lax.axis_size("col")
    vox_count = lax.axis_size("vox")
    row_pos = lax.axis_index("row")
    col_pos = lax.axis_index("col")
    vox_pos = lax.axis_index("vox")
    per_col = rhs.shape[0]
    rows = rhs.shape[2]
    voxels = rhs.shape[3]
    own = coeffs_r.shape[4]
    order = inverses.shape[1]
    tail = order // (rows * row_count)
    piece = tail * rows
    owner = col_count - 1
    where = jnp.stack([row_pos, vox_pos, (col_pos == owner).astype(jnp.int32)]).astype(jnp.int32)
    bf16 = jnp.bfloat16

    def gather_rows(value):
        pairs = [[(r, r ^ d) for r in range(row_count)] for d in range(row_count)]
        return [value] + [lax.ppermute(value, "row", pairs[d]) for d in range(1, row_count)]

    def step_down(value, step):
        stride = col_count >> (step + 1)
        targets = range(stride - 1, owner, 2 * stride)
        pairs = [(t + stride, t) for t in targets]
        if stride == 1:
            pairs += [(t, t + stride) for t in targets]
        got = lax.ppermute(value, "col", pairs)
        is_target = functools.reduce(jnp.logical_or, [col_pos == t for t in targets])
        return jnp.where(is_target, got, value)

    half = per_col // vox_count
    split = coeffs_r.reshape(col_count, vox_count, half * rows, 2, own)
    halves = lax.dynamic_slice_in_dim(split, vox_pos, 1, 1)[:, 0].transpose(2, 0, 1, 3)

    def spread_coeffs(which):
        return lax.all_to_all(halves[which], "col", 0, 0, tiled=True)

    def swap(value):
        return lax.ppermute(value, "vox", [(0, 1), (1, 0)])

    def scratch(width):
        return [pltpu.VMEM((order, width), bf16), pltpu.VMEM((order, width), bf16)]

    params = pltpu.CompilerParams(vmem_limit_bytes=12 << 20)

    def cost(width, n_rows):
        flops = 2 * order * width * (order + n_rows)
        return pl.CostEstimate(flops=flops, bytes_accessed=flops // 400, transcendentals=0)

    downs = col_count.bit_length() - 1
    mid_piece = rhs[per_col - 2 * tail : per_col - tail].reshape(piece, voxels)
    last_piece = rhs[per_col - tail :].reshape(piece, voxels)

    top = gather_rows(last_piece)
    spread = step_down(last_piece, 0)
    mine_1 = spread_coeffs(1)
    for s in range(1, downs):
        spread = step_down(spread, s)
    other_1 = swap(mine_1)

    mids = []
    for cols in chunk_bounds(voxels):
        width = cols.stop - cols.start
        mids.append(
            pl.pallas_call(
                functools.partial(mid_kernel, row_count, rows, (per_col - 2 * tail) * rows, cols),
                out_shape=jax.ShapeDtypeStruct((piece, width), bf16),
                in_specs=[SMEM] + [VMEM] * (row_count + 4),
                out_specs=VMEM,
                scratch_shapes=scratch(width),
                compiler_params=params,
                cost_estimate=cost(width, piece),
            )(where, *top, inverses, mine_1, other_1, mid_piece)
        )
    mids = [step_down(mid, 0) for mid in mids]
    last = gather_rows(spread)
    for s in range(1, downs):
        mids = [step_down(mid, s) for mid in mids]
    mine_0 = spread_coeffs(0)
    middle = [gather_rows(mid) for mid in mids]
    other_0 = swap(mine_0)

    flat = rhs.reshape(per_col * rows, voxels)
    acc, x_rows = pl.pallas_call(
        functools.partial(last_kernel, row_count, rows),
        out_shape=(jax.ShapeDtypeStruct(flat.shape, jnp.float32), jax.ShapeDtypeStruct((piece, voxels), bf16)),
        in_specs=[SMEM] + [VMEM] * (row_count + 4),
        out_specs=(VMEM, VMEM),
        scratch_shapes=scratch(voxels),
        compiler_params=params,
        cost_estimate=cost(voxels, per_col * rows),
        name="last",
    )(where, *last, inverses, mine_1, other_1, flat)
    pieces = [middle[n][d] for d in range(row_count) for n in range(CHUNKS)]
    out = pl.pallas_call(
        functools.partial(final_kernel, row_count, rows, CHUNKS),
        out_shape=jax.ShapeDtypeStruct(flat.shape, bf16),
        in_specs=[SMEM] + [VMEM] * (row_count * CHUNKS + 5),
        out_specs=VMEM,
        scratch_shapes=scratch(voxels),
        compiler_params=params,
        cost_estimate=cost(voxels, per_col * rows),
        name="final",
    )(where, *pieces, inverses, mine_0, other_0, acc, x_rows)
    return out.reshape(rhs.shape)


def solution(mesh):
    placed = (P(None, "row", None, None, "col"), P("col", "row", None, "vox"), P())

    return jax.shard_map(
        local, mesh=mesh, in_specs=placed, out_specs=P("col", "row", None, "vox"), check_vma=False
    )
```

```python
import functools

import jax
import jax.numpy as jnp
from jax import lax
from jax.experimental import pallas as pl
from jax.experimental.pallas import tpu as pltpu
from jax.sharding import PartitionSpec as P

BOTH = True
STEP = 256
VMEM = pl.BlockSpec(memory_space=pltpu.VMEM)
SMEM = pl.BlockSpec(memory_space=pltpu.SMEM)


def chunk_bounds(voxels):
    cut = voxels // 256 * 2 // 3 * 256 or voxels // 2
    return [slice(0, cut), slice(cut, voxels)]


def dot(a, b):
    return jnp.dot(a, b, preferred_element_type=jnp.float32)


def assemble(full, pieces, row_pos, rows):
    count = len(pieces)
    tail = pieces[0].shape[0] // rows
    for d, piece in enumerate(pieces):
        p = row_pos ^ d
        for k in range(tail):
            at = pl.multiple_of((k * count + p) * rows, rows)
            full[pl.ds(at, rows), :] = piece[k * rows : (k + 1) * rows, :]


def solve_step(x, inverse, full):
    step = inverse.shape[1]
    at = pl.multiple_of(pl.program_id(0) * step, step)
    x[pl.ds(at, step), :] = dot(inverse[0], full[...]).astype(x.dtype)


def first_step(f):
    pl.when(pl.program_id(0) == 0)(f)


def last_step(f):
    pl.when(pl.program_id(0) == pl.num_programs(0) - 1)(f)


def subtract(total, coeffs, x, at=slice(None)):
    own = coeffs.shape[2]
    for c in range(coeffs.shape[0]):
        total = total - dot(coeffs[c, at, :], x[c * own : (c + 1) * own, :])
    return total


def own_rows(x, row_pos, count, rows):
    tail = x.shape[0] // (count * rows)
    return [x[pl.ds(pl.multiple_of((k * count + row_pos) * rows, rows), rows), :] for k in range(tail)]


def mid_kernel(row_count, rows, start, cols, where, *refs):
    pieces = [ref.at[:, cols] for ref in refs[:row_count]]
    inverse, *halves, mid, out, full, x = refs[row_count:]
    half, piece = halves[0].shape[1], mid.shape[0]

    @pl.when(where[2] == 1)
    def _():
        first_step(lambda: assemble(full, pieces, where[0], rows))
        solve_step(x, inverse, full)

        @last_step
        def _():
            for h in range(2):
                low, high = max(start, h * half), min(start + piece, (h + 1) * half)
                if low >= high:
                    continue
                to = slice(low - start, high - start)

                def rest(coeffs):
                    total = mid[to, cols].astype(jnp.float32)
                    total = subtract(total, coeffs, x, slice(low - h * half, high - h * half))
                    out[to, :] = total.astype(out.dtype)

                if len(halves) == 1:
                    rest(halves[0])
                else:
                    pl.when(where[1] == h)(functools.partial(rest, halves[0]))
                    pl.when(where[1] != h)(functools.partial(rest, halves[1]))

    @pl.when(where[2] == 0)
    def _():
        out[...] = jnp.zeros_like(out)


def last_kernel(row_count, rows, where, *refs):
    pieces = refs[:row_count]
    inverse, mine, other, rhs, acc, x_rows, full, x = refs[row_count:]
    first_step(lambda: assemble(full, pieces, where[0], rows))
    solve_step(x, inverse, full)

    @last_step
    def _():
        for k, part in enumerate(own_rows(x, where[0], row_count, rows)):
            x_rows[k * rows : (k + 1) * rows, :] = part
        half = mine.shape[1]
        for coeffs, h in ((mine, where[1]), (other, 1 - where[1])):
            at = pl.multiple_of(h * half, half)
            acc[pl.ds(at, half), :] = subtract(rhs[pl.ds(at, half), :].astype(jnp.float32), coeffs, x)


def final_kernel(row_count, rows, cols, where, *refs):
    pieces = refs[:row_count]
    inverse, mine, other, acc, x_rows, *_, out, full, x = refs[row_count:]
    first_step(lambda: assemble(full, pieces, where[0], rows))
    solve_step(x, inverse, full)

    @last_step
    def _():
        half = mine.shape[1]
        for coeffs, h in ((mine, where[1]), (other, 1 - where[1])):
            at = pl.multiple_of(h * half, half)
            out[pl.ds(at, half), :] = subtract(acc[pl.ds(at, half), cols], coeffs, x).astype(out.dtype)

        @pl.when(where[2] == 1)
        def _():
            piece = x_rows.shape[0]
            start = out.shape[0] - 2 * piece
            for k, part in enumerate(own_rows(x, where[0], row_count, rows)):
                out[start + k * rows : start + (k + 1) * rows, :] = part
            out[start + piece :, :] = x_rows[:, cols]


def local(coeffs_r, rhs, inverses):
    row_count = lax.axis_size("row")
    col_count = lax.axis_size("col")
    vox_count = lax.axis_size("vox")
    row_pos = lax.axis_index("row")
    col_pos = lax.axis_index("col")
    vox_pos = lax.axis_index("vox")
    per_col = rhs.shape[0]
    rows = rhs.shape[2]
    voxels = rhs.shape[3]
    own = coeffs_r.shape[4]
    order = inverses.shape[1]
    tail = order // (rows * row_count)
    piece = tail * rows
    owner = col_count - 1
    where = jnp.stack([row_pos, vox_pos, (col_pos == owner).astype(jnp.int32)]).astype(jnp.int32)
    bf16 = jnp.bfloat16

    def gather_rows(value):
        pairs = [[(r, r ^ d) for r in range(row_count)] for d in range(row_count)]
        return [value] + [lax.ppermute(value, "row", pairs[d]) for d in range(1, row_count)]

    def take(value, got, targets):
        is_target = functools.reduce(jnp.logical_or, [col_pos == t for t in targets])
        return jnp.where(is_target, got, value)

    def step_down(value, step, both_ways=False):
        stride = col_count >> (step + 1)
        targets = list(range(stride - 1, owner, 2 * stride))
        if both_ways and len(targets) > 1:
            high = targets.pop()
            got = lax.ppermute(value, "col", [(high - stride, high)])
            lower = lax.ppermute(value, "col", [(t + stride, t) for t in targets])
            return take(take(value, lower, targets), got, [high])
        pairs = [(t + stride, t) for t in targets]
        if stride == 1:
            pairs += [(t, t + stride) for t in targets]
        return take(value, lax.ppermute(value, "col", pairs), targets)

    half = per_col // vox_count
    split = coeffs_r.reshape(col_count, vox_count, half * rows, 2, own)
    direct = per_col == 2 * tail
    mine = lax.dynamic_slice_in_dim(split, vox_pos, 1, 1)
    if direct:
        mine = jnp.concatenate([mine[:owner], split[owner:, :1]], 0)
    halves = mine[:, 0].transpose(2, 0, 1, 3)

    def spread_coeffs(which):
        return lax.all_to_all(halves[which], "col", 0, 0, tiled=True)

    def swap(value):
        return lax.ppermute(value, "vox", [(0, 1), (1, 0)])

    step = min(STEP, order)

    def call(body, args, specs, out_shape, out_specs, which, width, n_rows, aliases=None):
        flops = 2 * order * width * (order + n_rows)
        return pl.pallas_call(
            body,
            grid=(order // step,),
            out_shape=out_shape,
            in_specs=[SMEM] + [VMEM] * row_count + [pl.BlockSpec((1, step, order), lambda m: (which, m, 0))] + specs,
            out_specs=out_specs,
            scratch_shapes=[pltpu.VMEM((order, width), bf16), pltpu.VMEM((order, width), bf16)],
            input_output_aliases=aliases or {},
            compiler_params=pltpu.CompilerParams(vmem_limit_bytes=16 << 20),
            cost_estimate=pl.CostEstimate(flops=flops, bytes_accessed=flops // 400, transcendentals=0),
        )(where, *args)

    downs = col_count.bit_length() - 1
    bounds = chunk_bounds(voxels)
    mid_piece = rhs[per_col - 2 * tail : per_col - tail].reshape(piece, voxels)
    last_piece = rhs[per_col - tail :].reshape(piece, voxels)

    top = gather_rows(last_piece)
    spread = step_down(last_piece, 0)
    mine_1 = spread_coeffs(1)
    for s in range(1, downs):
        spread = step_down(spread, s, both_ways=BOTH)
    other_1 = swap(mine_1)
    panels = [mine_1] if direct else [mine_1, other_1]

    mids = []
    for cols in bounds:
        width = cols.stop - cols.start
        body = functools.partial(mid_kernel, row_count, rows, (per_col - 2 * tail) * rows, cols)
        shape = jax.ShapeDtypeStruct((piece, width), bf16)
        args = (*top, pltpu.with_memory_space_constraint(inverses, pltpu.HBM), *panels, mid_piece)
        mids.append(call(body, args, [VMEM] * (len(panels) + 1), shape, VMEM, 1, width, piece))
    mids = [step_down(mid, 0) for mid in mids]
    last = gather_rows(spread)
    for s in range(1, downs):
        mids = [step_down(mid, s) for mid in mids]
    mine_0 = spread_coeffs(0)
    middle = [gather_rows(mid) for mid in mids]
    other_0 = swap(mine_0)

    flat = rhs.reshape(per_col * rows, voxels)
    acc, x_rows = call(
        functools.partial(last_kernel, row_count, rows),
        (*last, inverses, mine_1, other_1, flat),
        [VMEM] * 3,
        (jax.ShapeDtypeStruct(flat.shape, jnp.float32), jax.ShapeDtypeStruct((piece, voxels), bf16)),
        (VMEM, VMEM),
        1,
        voxels,
        per_col * rows,
    )
    out = None
    for n, cols in enumerate(bounds):
        width = cols.stop - cols.start
        block = cols.start // width
        done = [] if out is None else [out]
        out = call(
            functools.partial(final_kernel, row_count, rows, cols),
            (*middle[n], inverses, mine_0, other_0, acc, x_rows, *done),
            [VMEM] * 4 + [pl.BlockSpec(memory_space=pl.ANY)] * len(done),
            jax.ShapeDtypeStruct(flat.shape, bf16),
            pl.BlockSpec((per_col * rows, width), functools.partial(lambda block, m: (0, block), block)),
            0,
            width,
            per_col * rows,
            {row_count + 6: 0} if done else None,
        )
    return out.reshape(rhs.shape)


def solution(mesh):
    placed = (P(None, "row", None, None, "col"), P("col", "row", None, "vox"), P())

    return jax.shard_map(local, mesh=mesh, in_specs=placed, out_specs=P("col", "row", None, "vox"), check_vma=False)
```

```python
import functools

import jax
import jax.numpy as jnp
from jax import lax
from jax.experimental import pallas as pl
from jax.experimental.pallas import tpu as pltpu
from jax.sharding import PartitionSpec as P

BOTH = False
STEP = 256
VMEM = pl.BlockSpec(memory_space=pltpu.VMEM)
SMEM = pl.BlockSpec(memory_space=pltpu.SMEM)


def chunk_bounds(voxels):
    cut = voxels // 256 * 2 // 3 * 256 or voxels // 2
    return [slice(0, cut), slice(cut, voxels)]


def dot(a, b):
    return jnp.dot(a, b, preferred_element_type=jnp.float32)


def assemble(full, pieces, row_pos, rows):
    count = len(pieces)
    tail = pieces[0].shape[0] // rows
    for d, piece in enumerate(pieces):
        p = row_pos ^ d
        for k in range(tail):
            at = pl.multiple_of((k * count + p) * rows, rows)
            full[pl.ds(at, rows), :] = piece[k * rows : (k + 1) * rows, :]


def blocks_of(rows):
    step = min(STEP, rows)
    return [slice(n * step, (n + 1) * step) for n in range(rows // step)]


def solve(x, full, pieces, row_pos, rows, inverses, which):
    assemble(full, pieces, row_pos, rows)
    for at in blocks_of(x.shape[0]):
        x[at, :] = dot(inverses[which, at, :], full[...]).astype(x.dtype)


def subtract(total, coeffs, x, at=slice(None), cols=slice(None)):
    own = coeffs.shape[2]
    for c in range(coeffs.shape[0]):
        total = total - dot(coeffs[c, at, :], x[c * own : (c + 1) * own, cols])
    return total


def own_rows(x, row_pos, count, rows):
    tail = x.shape[0] // (count * rows)
    return [x[pl.ds(pl.multiple_of((k * count + row_pos) * rows, rows), rows), :] for k in range(tail)]


def top_kernel(row_count, rows, where, *refs):
    pieces, (inverses, out, full, x, held, sems) = refs[:row_count], refs[row_count:]

    @pl.when(where[2] == 1)
    def _():
        blocks = blocks_of(x.shape[0])
        copies_in = [
            pltpu.make_async_copy(inverses.at[1, at, :], held.at[at, :], sems.at[0, n]) for n, at in enumerate(blocks)
        ]
        copies_out = [pltpu.make_async_copy(x.at[at, :], out.at[at, :], sems.at[1, n]) for n, at in enumerate(blocks)]
        for copy in copies_in:
            copy.start()
        assemble(full, pieces, where[0], rows)
        for at, copy_in, copy_out in zip(blocks, copies_in, copies_out):
            copy_in.wait()
            x[at, :] = dot(held[at, :], full[...]).astype(x.dtype)
            copy_out.start()
        for copy in copies_out:
            copy.wait()


def mid_kernel(start, bounds, where, *refs):
    count = len(bounds)
    solved, *halves, rhs = refs[: -2 - count]
    outs, (x, sems) = refs[-2 - count : -2], refs[-2:]
    half, piece = halves[0].shape[1], outs[0].shape[0]

    def rest(h, coeffs):
        low, high = max(start, h * half), min(start + piece, (h + 1) * half)
        to = slice(low - start, high - start)
        for cols, out in zip(bounds, outs):
            total = rhs[to, cols].astype(jnp.float32)
            total = subtract(total, coeffs, x, slice(low - h * half, high - h * half), cols)
            out[to, :] = total.astype(out.dtype)

    @pl.when(where[2] == 1)
    def _():
        copies = [
            pltpu.make_async_copy(solved.at[at, :], x.at[at, :], sems.at[n])
            for n, at in enumerate(blocks_of(x.shape[0]))
        ]
        for copy in copies:
            copy.start()
        for copy in copies:
            copy.wait()
        for h in range(2):
            if max(start, h * half) >= min(start + piece, (h + 1) * half):
                continue
            if len(halves) == 1:
                rest(h, halves[0])
            else:
                pl.when(where[1] == h)(functools.partial(rest, h, halves[0]))
                pl.when(where[1] != h)(functools.partial(rest, h, halves[1]))

    @pl.when(where[2] == 0)
    def _():
        for out in outs:
            out[...] = jnp.zeros_like(out)


def last_kernel(row_count, rows, where, *refs):
    pieces = refs[:row_count]
    inverse, mine, other, rhs, acc, x_rows, full, x = refs[row_count:]
    solve(x, full, pieces, where[0], rows, inverse, 1)
    for k, part in enumerate(own_rows(x, where[0], row_count, rows)):
        x_rows[k * rows : (k + 1) * rows, :] = part
    half = mine.shape[1]
    for coeffs, h in ((mine, where[1]), (other, 1 - where[1])):
        at = pl.multiple_of(h * half, half)
        acc[pl.ds(at, half), :] = subtract(rhs[pl.ds(at, half), :].astype(jnp.float32), coeffs, x)


def final_kernel(row_count, rows, cols, where, *refs):
    pieces = refs[:row_count]
    inverse, mine, other, acc, x_rows, *_, out, full, x = refs[row_count:]
    solve(x, full, pieces, where[0], rows, inverse, 0)
    half = mine.shape[1]
    for coeffs, h in ((mine, where[1]), (other, 1 - where[1])):
        at = pl.multiple_of(h * half, half)
        out[pl.ds(at, half), :] = subtract(acc[pl.ds(at, half), cols], coeffs, x).astype(out.dtype)

    @pl.when(where[2] == 1)
    def _():
        piece = x_rows.shape[0]
        start = out.shape[0] - 2 * piece
        for k, part in enumerate(own_rows(x, where[0], row_count, rows)):
            out[start + k * rows : start + (k + 1) * rows, :] = part
        out[start + piece :, :] = x_rows[:, cols]


def local(coeffs_r, rhs, inverses):
    row_count = lax.axis_size("row")
    col_count = lax.axis_size("col")
    vox_count = lax.axis_size("vox")
    row_pos = lax.axis_index("row")
    col_pos = lax.axis_index("col")
    vox_pos = lax.axis_index("vox")
    per_col = rhs.shape[0]
    rows = rhs.shape[2]
    voxels = rhs.shape[3]
    own = coeffs_r.shape[4]
    order = inverses.shape[1]
    tail = order // (rows * row_count)
    piece = tail * rows
    owner = col_count - 1
    where = jnp.stack([row_pos, vox_pos, (col_pos == owner).astype(jnp.int32)]).astype(jnp.int32)
    bf16 = jnp.bfloat16

    def gather_rows(value):
        pairs = [[(r, r ^ d) for r in range(row_count)] for d in range(row_count)]
        return [value] + [lax.ppermute(value, "row", pairs[d]) for d in range(1, row_count)]

    def take(value, got, targets):
        is_target = functools.reduce(jnp.logical_or, [col_pos == t for t in targets])
        return jnp.where(is_target, got, value)

    def step_down(value, step, both_ways=False):
        stride = col_count >> (step + 1)
        targets = list(range(stride - 1, owner, 2 * stride))
        if both_ways and len(targets) > 1:
            high = targets.pop()
            got = lax.ppermute(value, "col", [(high - stride, high)])
            lower = lax.ppermute(value, "col", [(t + stride, t) for t in targets])
            return take(take(value, lower, targets), got, [high])
        pairs = [(t + stride, t) for t in targets]
        if stride == 1:
            pairs += [(t, t + stride) for t in targets]
        return take(value, lax.ppermute(value, "col", pairs), targets)

    half = per_col // vox_count
    split = coeffs_r.reshape(col_count, vox_count, half * rows, 2, own)
    direct = per_col == 2 * tail
    mine = lax.dynamic_slice_in_dim(split, vox_pos, 1, 1)
    if direct:
        mine = jnp.concatenate([mine[:owner], split[owner:, :1]], 0)
    halves = mine[:, 0].transpose(2, 0, 1, 3)

    def spread_coeffs(which):
        return lax.all_to_all(halves[which], "col", 0, 0, tiled=True)

    def swap(value):
        return lax.ppermute(value, "vox", [(0, 1), (1, 0)])

    HBM = pl.BlockSpec(memory_space=pltpu.HBM)
    blocks = len(blocks_of(order))

    def call(body, args, specs, out_shape, out_specs, width, n_rows, aliases=None, scratch=None):
        flops = 2 * order * width * (order + n_rows)
        return pl.pallas_call(
            body,
            out_shape=out_shape,
            grid=(1,),
            in_specs=[SMEM] + specs,
            out_specs=out_specs,
            scratch_shapes=scratch or [pltpu.VMEM((order, width), bf16)] * 2,
            input_output_aliases=aliases or {},
            compiler_params=pltpu.CompilerParams(vmem_limit_bytes=8 << 20),
            cost_estimate=pl.CostEstimate(flops=flops, bytes_accessed=flops // 400, transcendentals=0),
        )(where, *args)

    downs = col_count.bit_length() - 1
    bounds = chunk_bounds(voxels)
    flat = rhs.reshape(per_col * rows, voxels)
    last_piece = rhs[per_col - tail :].reshape(piece, voxels)
    mid_piece = rhs[per_col - 2 * tail : per_col - tail].reshape(piece, voxels)

    top = gather_rows(last_piece)
    spread = step_down(last_piece, 0)
    mine_1 = spread_coeffs(1)
    for s in range(1, downs):
        spread = step_down(spread, s, both_ways=BOTH)
    other_1 = swap(mine_1)
    panels = [mine_1] if direct else [mine_1, other_1]

    x_top = call(
        functools.partial(top_kernel, row_count, rows),
        (*top, pltpu.with_memory_space_constraint(inverses, pltpu.HBM)),
        [VMEM] * row_count + [HBM],
        pltpu.HBM((order, voxels), bf16),
        HBM,
        voxels,
        0,
        scratch=[
            pltpu.VMEM((order, voxels), bf16),
            pltpu.VMEM((order, voxels), bf16),
            pltpu.VMEM((order, order), bf16),
            pltpu.SemaphoreType.DMA((2, blocks)),
        ],
    )
    args = (pltpu.with_memory_space_constraint(x_top, pltpu.HBM), *panels, mid_piece)
    mids = call(
        functools.partial(mid_kernel, (per_col - 2 * tail) * rows, bounds),
        args,
        [HBM] + [VMEM] * (len(args) - 1),
        [jax.ShapeDtypeStruct((piece, cols.stop - cols.start), bf16) for cols in bounds],
        [VMEM] * len(bounds),
        voxels,
        0,
        scratch=[pltpu.VMEM((order, voxels), bf16), pltpu.SemaphoreType.DMA((blocks,))],
    )
    mids = [step_down(mid, 0) for mid in mids]
    last = gather_rows(spread)
    for s in range(1, downs):
        mids = [step_down(mid, s) for mid in mids]
    mine_0 = spread_coeffs(0)
    middle = [gather_rows(mid) for mid in mids]
    other_0 = swap(mine_0)

    acc, x_rows = call(
        functools.partial(last_kernel, row_count, rows),
        (*last, inverses, mine_1, other_1, flat),
        [VMEM] * (row_count + 4),
        (jax.ShapeDtypeStruct(flat.shape, jnp.float32), jax.ShapeDtypeStruct((piece, voxels), bf16)),
        (VMEM, VMEM),
        voxels,
        per_col * rows,
    )
    out = None
    for n, cols in enumerate(bounds):
        width = cols.stop - cols.start
        block = cols.start // width
        done = [] if out is None else [out]
        out = call(
            functools.partial(final_kernel, row_count, rows, cols),
            (*middle[n], inverses, mine_0, other_0, acc, x_rows, *done),
            [VMEM] * (row_count + 5) + [pl.BlockSpec(memory_space=pl.ANY)] * len(done),
            jax.ShapeDtypeStruct(flat.shape, bf16),
            pl.BlockSpec((per_col * rows, width), functools.partial(lambda block, m: (0, block), block)),
            width,
            per_col * rows,
            {row_count + 6: 0} if done else None,
        )
    return out.reshape(rhs.shape)


def solution(mesh):
    placed = (P(None, "row", None, None, "col"), P("col", "row", None, "vox"), P())

    return jax.shard_map(local, mesh=mesh, in_specs=placed, out_specs=P("col", "row", None, "vox"), check_vma=False)
```
